32 devices in a mesh: groups: 2 (over y), tm: 16 (over z, x, core).
Axes of the slice: x: 2, y: 2, z: 4, core: 2. Of those that a mesh axis runs over, the one named last changes fastest.
Arguments:
- slot_frames: bfloat16 [256, 128, 1536], P(('groups', 'tm')), parts along dimension 0, may hold values from -6 to 6
- slot_live: int32 [256], P(('groups', 'tm')), parts along dimension 0, may hold values from 0 to 1, as said below
- utterance_start: int32 [4, 4096], P('groups', 'tm'), parts along dimension 0, may hold values from 0 to 4095, as said below
- in_projection: bfloat16 [1536, 2304], P('tm'), may hold values from -4 to 4, as said below
- out_projection: bfloat16 [768, 1536], P('tm'), may hold values from -0.21875 to 0.21875
- pointwise_in: bfloat16 [1536, 1536], P('tm'), may hold values from -0.15625 to 0.15625
- depthwise: float32 [31, 768], replicated, may hold values from -1 to 1
- pointwise_out: bfloat16 [768, 1536], P('tm'), may hold values from -0.21875 to 0.21875
- gain_attention: float32 [1536], replicated, may hold values from 0.25 to 1.75
- gain_convolution: float32 [1536], replicated, may hold values from 0.25 to 1.75
- gain_depth: float32 [768], replicated, may hold values from 0.25 to 1.75
Outputs:
- block_output: bfloat16 [4, 4096, 1536], P('groups', 'tm'), parts along dimension 0
The draws below stay inside these ranges and needn't reach their ends.
There are 2 independent parts, one for each index of `groups`. The reference program is written for one: setup_inputs(seed, part) draws one part's arguments, and reference() takes and returns one part's arrays. A program takes and returns all parts, laid end to end along the dimension named above; an argument that names none is the same for every part. Nothing has to cross between parts.
Inputs may be any that keep to these rules, and one draw needn't show every extreme that they name: `slot_live`: with P(d) the number of live slots on time shards 0 to d - 1: 4 * (d - 2) <= P(d) <= 4 * (d + 2) for every d, both ends reached, and the whole group has exactly 4 live slots per time shard. A time shard has 0 to 8 live slots. utterance_start[s, t] <= t, never falls along t, and equals t where an utterance begins; it is 0 at t = 0. `in_projection`: entries of order 1 / sqrt(1536) or larger.
All inputs are finite; a program needn't handle non-finite values.
Results may differ from the reference program's by a relative error of at most 0.007.
Values may be sent and summed in bfloat16 or wider, within the bound.
No kernel may reach another device: no remote copies, remote signals or barrier semaphores. Data moves between devices by JAX's collectives and lax.ppermute only.
A program may use at most 128 MiB of HBM per device.

```python
import math
import jax
import jax.numpy as jnp
from jax import lax

D = 1536
H = 8
HD = 96
CH = 768
KERNEL = 31
CTX = 256
BLK = 128
STREAMS = 2
T_DEV = 256
BPO = 4
SLOTS = 8
TIME = 4096
N_TM = 16


def draw_slot_live(key, part):
    owner_blocks = BPO
    first_key, second_key = jax.random.split(jax.random.fold_in(key, 11))
    rolls = jax.random.randint(first_key, (N_TM,), 0, 1 << 20)

    def advance(excess, item):
        device, roll = item
        lowest = jnp.maximum(0, -owner_blocks - excess)
        highest = jnp.minimum(2 * owner_blocks, 3 * owner_blocks - excess)
        count_now = lowest + roll % (highest - lowest + 1)
        count_now = jnp.where(device < 2, 2 * owner_blocks, count_now)
        count_now = jnp.where((device >= 2) & (device < 6), 0, count_now)
        half_excess = jnp.floor_divide(excess, 2)
        count_now = jnp.where(device == N_TM - 2, owner_blocks - half_excess, count_now)
        count_now = jnp.where(device == N_TM - 1, owner_blocks - excess, count_now)
        return (excess + count_now - owner_blocks, count_now)
    final_excess, counts = lax.scan(advance, jnp.int32(0), (jnp.arange(N_TM, dtype=jnp.int32), rolls))
    scores = jax.random.randint(second_key, (N_TM, SLOTS), 0, 1 << 16) * SLOTS + jnp.arange(SLOTS, dtype=jnp.int32)[None, :]
    ranks = jnp.argsort(jnp.argsort(scores, axis=1), axis=1)
    return (ranks < counts[:, None]).astype(jnp.int32).reshape(N_TM * SLOTS)


def draw_utterance_start(key, part):
    frames = jnp.arange(TIME, dtype=jnp.int32)
    rolls = jax.random.randint(jax.random.fold_in(key, 23), (STREAMS, TIME), 0, 320)
    begins = (rolls == 0) | (frames[None, :] == 0) | (frames[None, :] == TIME - 1)
    return lax.cummax(jnp.where(begins, frames[None, :], 0), axis=1)


def draw_in_projection(key, part):
    first_key = jax.random.fold_in(jax.random.fold_in(key, 37), 0)
    stacked = jnp.clip(jax.random.normal(first_key, (D, 3, H, HD), jnp.float32), -6.0, 6.0) * D ** (-0.5)
    return stacked.reshape(D, 3 * H * HD).astype(jnp.bfloat16)


def block_scale(stream_key, extent, pieces, low, largest):
    def one(dim, shards_of):
        steps = jax.random.uniform(jax.random.fold_in(jax.random.fold_in(stream_key, 6), dim), (shards_of,), jnp.float32, low / len(pieces), largest / len(pieces))
        return jnp.repeat(jnp.exp(steps), extent[dim] // shards_of).reshape((-1,) + (1,) * (len(extent) - dim - 1))

    factor_of = one(*pieces[0])
    for cut in pieces[1:]:
        factor_of = factor_of * one(*cut)
    return factor_of


def scatter_about(rng, shape, scale, limit, cuts=(), kind=jnp.bfloat16):
    array = jax.random.normal(rng, shape, jnp.float32) * scale
    if len(cuts) > 0:
        array = block_scale(rng, shape, cuts, -0.22, 0.18) * array
    return jnp.clip(array, min=-limit, max=limit).astype(kind)


def setup_inputs(seed: int = 0, part: int = 0) -> dict:
    key_of = jax.random.split(jax.random.key(seed), 12)
    own_keys = jax.random.split(jax.random.fold_in(key_of[11], part), 12)
    return {
        "slot_frames": scatter_about(own_keys[0], (N_TM * SLOTS, BLK, D), 1.0, 6.0, ((0, 16),)),
        "slot_live": draw_slot_live(jax.random.fold_in(jax.random.fold_in(key_of[11], part), 71), part),
        "utterance_start": draw_utterance_start(jax.random.fold_in(jax.random.fold_in(key_of[11], part), 71), part),
        "in_projection": draw_in_projection(jax.random.fold_in(key_of[11], 71), part),
        "out_projection": scatter_about(key_of[4], (H * HD, D), (H * HD) ** -0.5, 0.21875, ((0, 16),)),
        "pointwise_in": scatter_about(key_of[5], (D, 2 * CH), D ** -0.5, 0.15625, ((0, 16),)),
        "depthwise": scatter_about(key_of[6], (KERNEL, CH), KERNEL ** -0.5, 1.0, (), jnp.float32),
        "pointwise_out": scatter_about(key_of[7], (CH, D), CH ** -0.5, 0.21875, ((0, 16),)),
        "gain_attention": jnp.clip(1.0 + 0.15 * jax.random.normal(key_of[8], (D,), jnp.float32), 0.25, 1.75),
        "gain_convolution": jnp.clip(1.0 + 0.15 * jax.random.normal(key_of[9], (D,), jnp.float32), 0.25, 1.75),
        "gain_depth": jnp.clip(1.0 + 0.15 * jax.random.normal(key_of[10], (CH,), jnp.float32), 0.25, 1.75),
    }


epsilon = 1e-05

def layer_norm(values, gain_row):
    center = values - lax.optimization_barrier(jnp.mean(values, axis=-1, keepdims=True))
    spread = lax.optimization_barrier(jnp.mean(center * center, axis=-1, keepdims=True))
    return center * lax.rsqrt(spread + epsilon) * gain_row

def reference(slot_frames, slot_live, utterance_start, in_projection, out_projection, pointwise_in, depthwise, pointwise_out, gain_attention, gain_convolution, gain_depth):
    owner_blocks = 2 * STREAMS
    all_blocks = N_TM * owner_blocks
    live_order = jnp.cumsum(slot_live) - 1
    target = jnp.where(slot_live > 0, live_order, all_blocks).astype(jnp.int32)
    placed = jnp.zeros((all_blocks + 1, BLK, D), jnp.bfloat16).at[target].set(slot_frames)[:all_blocks]
    stream = placed.reshape(N_TM, STREAMS, 2, BLK, D).transpose(1, 0, 2, 3, 4).reshape(STREAMS, TIME, D)
    normed = layer_norm(stream.astype(jnp.float32), gain_attention).astype(jnp.bfloat16)
    projected = jnp.dot(normed.reshape(STREAMS * TIME, D), in_projection, preferred_element_type=jnp.float32)
    projected = projected.astype(jnp.bfloat16).reshape(STREAMS, TIME, 3, H, HD)
    queries = projected[:, :, 0]
    key_rows = jnp.pad(projected[:, :, 1], ((0, 0), (T_DEV, 0), (0, 0), (0, 0)))
    value_rows = jnp.pad(projected[:, :, 2], ((0, 0), (T_DEV, 0), (0, 0), (0, 0)))
    scale_factor = 1.0 / math.sqrt(HD)

    def one_shard(shard_number):
        first_frame = shard_number * T_DEV
        query_part = lax.dynamic_slice_in_dim(queries, first_frame, T_DEV, 1).astype(jnp.float32)
        key_part = lax.dynamic_slice_in_dim(key_rows, first_frame, 2 * T_DEV, 1).astype(jnp.float32)
        value_part = lax.dynamic_slice_in_dim(value_rows, first_frame, 2 * T_DEV, 1).astype(jnp.float32)
        start_part = lax.dynamic_slice_in_dim(utterance_start, first_frame, T_DEV, 1)
        query_pos = first_frame + jnp.arange(T_DEV, dtype=jnp.int32)
        key_pos = first_frame - T_DEV + jnp.arange(2 * T_DEV, dtype=jnp.int32)
        allowed = (key_pos[None, None, :] <= query_pos[None, :, None]) & (key_pos[None, None, :] >= query_pos[None, :, None] - CTX) & (key_pos[None, None, :] >= start_part[:, :, None])
        scores = jnp.einsum('sqhd,skhd->shqk', query_part, key_part) * scale_factor
        scores = jnp.where(allowed[:, None], scores, -jnp.inf)
        row_peak = lax.optimization_barrier(jnp.max(scores, axis=-1, keepdims=True))
        raised = jnp.exp(scores - row_peak)
        weights = (raised / lax.optimization_barrier(jnp.sum(raised, axis=-1, keepdims=True))).astype(jnp.bfloat16)
        mixed_heads = jnp.einsum('shqk,skhd->sqhd', weights.astype(jnp.float32), value_part)
        return mixed_heads.astype(jnp.bfloat16).reshape(STREAMS, T_DEV, H * HD)
    shards = lax.map(one_shard, jnp.arange(N_TM, dtype=jnp.int32))
    mixed_heads = shards.transpose(1, 0, 2, 3).reshape(STREAMS * TIME, H * HD)
    attended = jnp.dot(mixed_heads, out_projection, preferred_element_type=jnp.float32)
    middle = (stream.reshape(STREAMS * TIME, D).astype(jnp.float32) + attended).astype(jnp.bfloat16)
    conv_in = layer_norm(middle.astype(jnp.float32), gain_convolution).astype(jnp.bfloat16)
    expanded = jnp.dot(conv_in, pointwise_in, preferred_element_type=jnp.float32)
    gated_rows = (expanded[:, :CH] * jax.nn.sigmoid(expanded[:, CH:])).astype(jnp.bfloat16).reshape(STREAMS, TIME, CH)
    padded = jnp.pad(gated_rows, ((0, 0), (KERNEL - 1, 0), (0, 0))).astype(jnp.float32)
    elapsed = jnp.arange(TIME, dtype=jnp.int32)[None, :] - utterance_start
    depth_sum = jnp.zeros((STREAMS, TIME, CH), jnp.float32)
    for tap_index in range(KERNEL):
        delay_rows = KERNEL - 1 - tap_index
        tap_term = padded[:, tap_index:tap_index + TIME] * depthwise[tap_index]
        depth_sum = depth_sum + jnp.where((elapsed >= delay_rows)[:, :, None], tap_term, 0.0)
    normed_depth = layer_norm(depth_sum, gain_depth)
    swished = (normed_depth * jax.nn.sigmoid(normed_depth)).astype(jnp.bfloat16).reshape(STREAMS * TIME, CH)
    output = middle.astype(jnp.float32) + jnp.dot(swished, pointwise_out, preferred_element_type=jnp.float32)
    return output.astype(jnp.bfloat16).reshape(STREAMS, TIME, D)
```

```python
import math

import jax
import jax.numpy as jnp
from jax import lax
from jax.experimental import pallas as pl
from jax.experimental.pallas import tpu as pltpu
from jax.sharding import PartitionSpec as P

H = 8
HD = 96
KERNEL = 31
CTX = 256
CHUNKS = 2
EDGE = 32
VMEM_LIMIT = 56 << 20

epsilon = 1e-05
bf16 = jnp.bfloat16
f32 = jnp.float32

ANY = pl.BlockSpec(memory_space=pl.ANY)
SMEM = pl.BlockSpec(memory_space=pltpu.SMEM)
VMEM = pl.BlockSpec(memory_space=pltpu.VMEM)


def layer_norm(values, gain_row):
    center = values - jnp.mean(values, axis=-1, keepdims=True)
    spread = jnp.mean(center * center, axis=-1, keepdims=True)
    return center * lax.rsqrt(spread + epsilon) * gain_row


def params():
    return pltpu.CompilerParams(vmem_limit_bytes=VMEM_LIMIT)


def after(value, *earlier):
    return lax.optimization_barrier((value, *earlier))[0]


def whole_weight(index):
    return [(index, side, lambda t: 0, lambda g, side=side: side) for side in (0, 1)]


def piece_copies():
    copies = []
    for flip, base in ((0, 0), (1, 5)):
        for side in (0, 1):
            copies.append((base, side, lambda t, f=flip: t ^ f, lambda g, s=side: s))
        for k in (1, 2, 3):
            plain = lambda t, k=k, f=flip: ((t - 4 * k) & 15) ^ f
            crossed = lambda t, k=k, f=flip: ((t - 4 * k) & 15) ^ (2 + f)
            copies.append((base + 1, k - 1, plain, lambda g: g))
            copies.append((base + 2, k - 1, crossed, lambda g: g))
            copies.append((base + 3, k - 1, plain, lambda g: 1 - g))
            copies.append((base + 4, k - 1, crossed, lambda g: 1 - g))
        next_door = lambda t, f=flip: t ^ (2 + f)
        copies.append((base + 1, 3, next_door, lambda g: g))
        copies.append((base + 3, 3, next_door, lambda g: 1 - g))
    return copies


def rest_pieces(parts, shift=0):
    pieces = []
    for part in range(parts):
        block = lambda t, part=part: part
        pieces.append((0, part, block, lambda g: g, lambda t: 0, shift))
        pieces.append((1, part, block, lambda g: 1 - g, lambda t: t & 1, 0))
        pieces.append((2, part, block, lambda g: 1 - g, lambda t: 1 - (t & 1), 0))
    return pieces


def load_weight(refs, pieces, segments, rows, place, target, sems):
    t, g = place
    started = []
    for array, lead, block, side, *quarter in pieces:
        for row, count, column, columns, row_offset, column_offset in segments:
            source = refs[array].at[lead]
            row = row + quarter[1] if quarter else row
            columns = source.shape[1] if columns is None else columns
            source = source.at[pl.ds(row, count), pl.ds(column, columns)]
            first = block(t)
            first = first * rows if isinstance(first, int) else pl.multiple_of(first * rows, rows)
            if quarter:
                column_offset = quarter[0](t)
                if not isinstance(column_offset, int):
                    column_offset = pl.multiple_of(column_offset * columns, 128)
            spot = target.at[side(g), pl.ds(first + row_offset, count), pl.ds(column_offset, columns)]
            copy = pltpu.make_async_copy(source, spot, sems.at[len(started)])
            copy.start()
            started.append(copy)
    return started


def prepare_kernel(place_ref, w_in, w_out, w_expand, w_last, half, half_rest, whole, sems):
    g = place_ref[1]
    width = half.shape[1]
    rows, columns = w_in.shape
    columns = columns // 2
    over = columns - width
    copies = []
    for target, side in ((half, g), (whole.at[0], 0), (whole.at[1], 1)):

        def lanes(base, size, side=side):
            return pl.ds(base if isinstance(side, int) else pl.multiple_of(base, 128), size)

        copies.append((w_in.at[:, lanes(side * columns, width)], target.at[pl.ds(0, rows)]))
        for part in (0, 1):
            source = w_in.at[pl.ds(part * rows // 2, rows // 2), lanes(side * columns + width, over)]
            copies.append((source, target.at[pl.ds(rows, rows // 2), pl.ds(part * over, over)]))
    row = 0
    for source in (w_out, w_expand, w_last):
        count = source.shape[0]
        copies.append((source.at[:, pl.ds(pl.multiple_of(g * width, 128), width)], half_rest.at[pl.ds(row, count)]))
        row += count
    started = [pltpu.make_async_copy(a, b, sems.at[i]) for i, (a, b) in enumerate(copies)]
    for copy in started:
        copy.start()
    for copy in started:
        copy.wait()


def hand_over_kernel(place_ref, frames, theirs, sem):
    part = theirs.shape[2]
    column = pl.multiple_of((1 - (place_ref[0] & 1)) * part, 128)
    copy = pltpu.make_async_copy(frames.at[:, :, pl.ds(column, part)], theirs, sem)
    copy.start()
    copy.wait()


def route_kernel(slots, chips, per_chunk, place_ref, live_ref, frames, theirs, *rest):
    chunks = rest[:CHUNKS]
    table_ref, leave_ref, sems = rest[CHUNKS:]
    t = place_ref[0]
    core = t & 1
    chip = t >> 1
    chip_slots = 2 * slots
    count = chip_slots // 2
    part = theirs.shape[2]
    mine = frames.at[:, :, pl.ds(pl.multiple_of(core * part, 128), part)]

    for j in range(count):
        table_ref[j] = 0
        leave_ref[j] = 0
    first = jnp.maximum(chip - 1, 0)
    total = lax.fori_loop(0, first * chip_slots, lambda f, s: s + live_ref[f], jnp.int32(0))

    for step in (-1, 0, 1):
        here = chip + step
        inside = (here >= 0) & (here < chips)
        start = jnp.clip(here, 0, chips - 1) * chip_slots
        if step == 0:
            offset = jnp.int32(0)
        else:
            offset = jnp.where(here == (chip ^ 1), chip_slots, chip_slots + count)

        def one(s, carry, step=step, here=here, inside=inside, start=start, offset=offset):
            counted, rank = carry
            live = jnp.where(inside, live_ref[start + s], 0)
            owner = counted // count
            leaving = jnp.where((live > 0) & (owner != here), 1, 0)

            @pl.when((live > 0) & (owner == chip))
            def _():
                table_ref[counted & (count - 1)] = (s if step == 0 else rank & (count - 1)) + offset

            if step == 0:

                @pl.when(leaving > 0)
                def _():
                    leave_ref[rank & (count - 1)] = s

            return counted + live, rank + leaving

        total, _ = lax.fori_loop(0, chip_slots, one, (total, jnp.int32(0)))
    for j in range(count):
        s = leave_ref[j]
        spot = chunks[j // per_chunk].at[j % per_chunk]
        own = (s // slots) == core

        @pl.when(own)
        def _():
            pltpu.make_async_copy(mine.at[s & (slots - 1)], spot, sems.at[j]).start()

        @pl.when(jnp.logical_not(own))
        def _():
            pltpu.make_async_copy(theirs.at[s & (slots - 1)], spot, sems.at[j]).start()

    for j in range(count):
        spot = chunks[j // per_chunk].at[j % per_chunk]
        pltpu.make_async_copy(mine.at[0], spot, sems.at[j]).wait()


def assemble_kernel(slots, per_chunk, place_ref, table_ref, frames, theirs, *rest):
    beside = rest[:CHUNKS]
    beyond = rest[CHUNKS : 2 * CHUNKS]
    keep, give, sems = rest[2 * CHUNKS :]
    core = place_ref[0] & 1
    part = theirs.shape[2]
    mine = frames.at[:, :, pl.ds(pl.multiple_of(core * part, 128), part)]
    count = slots
    blocks = count // 2
    for j in range(blocks):
        for side in (0, 1):
            target = (keep if side == 0 else give).at[j]
            sem = sems.at[side * blocks + j]
            code = table_ref[j + blocks * (core if side == 0 else 1 - core)]
            low = code & (slots - 1)
            local = code < 2 * slots
            own = (code // slots) == core

            @pl.when(local & own)
            def _():
                pltpu.make_async_copy(mine.at[low], target, sem).start()

            @pl.when(local & jnp.logical_not(own))
            def _():
                pltpu.make_async_copy(theirs.at[low], target, sem).start()

            for chunk in range(CHUNKS):
                for which, source in ((0, beside[chunk]), (1, beyond[chunk])):
                    low_end = 2 * slots + which * count + chunk * per_chunk

                    @pl.when((code >= low_end) & (code < low_end + per_chunk))
                    def _():
                        pltpu.make_async_copy(source.at[low & (per_chunk - 1)], target, sem).start()

    for j in range(blocks):
        pltpu.make_async_copy(mine.at[0], keep.at[j], sems.at[j]).wait()
        pltpu.make_async_copy(mine.at[0], give.at[j], sems.at[blocks + j]).wait()


def qkv_kernel(copies, segments, rows, place_ref, keep, other, gain, *rest):
    count = len(rest) - 6
    refs = rest[:count]
    stream, q, kv, weight, normed, sems = rest[count:]
    k, v = kv.at[0], kv.at[1]
    t, g = place_ref[0], place_ref[1]
    core = t & 1
    half = weight.shape[2]
    started = load_weight(refs, copies, segments, rows, (t, g), weight, sems)
    blocks, block_rows, part = keep.shape
    for b in range(blocks):
        a, o = keep[b], other[b]
        low = jnp.where(core == 0, a, o)
        high = jnp.where(core == 0, o, a)
        here = pl.ds(b * block_rows, block_rows)
        stream[here, pl.ds(0, part)] = low
        stream[here, pl.ds(part, part)] = high
        x = jnp.concatenate([low, high], axis=-1).astype(f32)
        normed[here] = layer_norm(x, gain[...]).astype(bf16)
    for copy in started:
        copy.wait()
    width = H * HD
    over = half - width
    tile = 256
    for b in range(blocks * block_rows // tile):
        here = pl.ds(b * tile, tile)
        x = normed[here]
        left = jnp.dot(x, weight[0], preferred_element_type=f32).astype(bf16)
        q[here] = left[:, :width]
        k[here, pl.ds(0, over)] = left[:, width:]
        right = jnp.dot(x, weight[1], preferred_element_type=f32).astype(bf16)
        k[here, pl.ds(over, width - over)] = right[:, : width - over]
        v[here] = right[:, width - over :]


def attention_kernel(frames, place_ref, q, kv, prior, starts, mixed, keys, values):
    k, v, prior_k, prior_v = kv.at[0], kv.at[1], prior.at[0], prior.at[1]
    t = place_ref[0]
    streams = q.shape[0] // frames
    tile = 128
    window = tile + CTX
    for s in range(streams):
        keys[pl.ds(2 * s * frames, frames)] = prior_k[pl.ds(s * frames, frames)]
        keys[pl.ds((2 * s + 1) * frames, frames)] = k[pl.ds(s * frames, frames)]
        values[pl.ds(2 * s * frames, frames)] = prior_v[pl.ds(s * frames, frames)]
        values[pl.ds((2 * s + 1) * frames, frames)] = v[pl.ds(s * frames, frames)]
    scale = 1.0 / math.sqrt(HD) / math.log(2.0)
    tiles = frames // tile

    def body(step, carry):
        s = step // tiles
        part = step % tiles
        here = pl.ds(pl.multiple_of(step * tile, tile), tile)
        there = pl.ds(pl.multiple_of(s * 2 * frames + part * tile, tile), window)
        row = lax.broadcasted_iota(jnp.int32, (tile, window), 0)
        col = lax.broadcasted_iota(jnp.int32, (tile, window), 1)
        begin = starts[here] - (t - 1) * frames - part * tile
        bias = jnp.where((col <= row + CTX) & (col >= row) & (col >= begin), 0.0, -1e30).astype(f32)
        for group in range(H // 4):
            outs = []
            for head in range(4):
                lane0 = head * HD
                first = lane0 // 128 * 128
                last = -(-(lane0 + HD) // 128) * 128
                lanes = pl.ds(group * 4 * HD + first, last - first)
                qs = q[here, lanes]
                lane = lax.broadcasted_iota(jnp.int32, qs.shape, 1) + first
                qs = jnp.where((lane >= lane0) & (lane < lane0 + HD), qs, jnp.zeros_like(qs))
                scores = lax.dot_general(
                    qs, keys[there, lanes], (((1,), (1,)), ((), ())), preferred_element_type=f32
                )
                scores = scores * scale + bias
                raised = jnp.exp2(scores - jnp.max(scores, axis=-1, keepdims=True))
                total = jnp.sum(raised, axis=-1, keepdims=True)
                out = jnp.dot(raised.astype(bf16), values[there, lanes], preferred_element_type=f32)
                outs.append(out * (1.0 / total))
            lane = lax.broadcasted_iota(jnp.int32, (tile, 128), 1)
            base = group * 4 * HD
            mixed[here, pl.ds(base, 128)] = jnp.where(lane < 96, outs[0], outs[1][:, :128]).astype(bf16)
            mixed[here, pl.ds(base + 128, 128)] = jnp.where(lane < 64, outs[1][:, 128:], outs[2][:, :128]).astype(
                bf16
            )
            mixed[here, pl.ds(base + 256, 128)] = jnp.where(lane < 32, outs[2][:, 128:], outs[3]).astype(bf16)
        return carry

    lax.fori_loop(0, streams * tiles, body, 0)


def gate_kernel(out_plan, in_plan, frames, place_ref, mixed, stream, gain, *rest):
    count = len(rest) - 7
    refs = rest[:count]
    middle, gated, edge, out_w, in_w, out_sems, in_sems = rest[count:]
    t, g = place_ref[0], place_ref[1]
    half = out_w.shape[2]
    out_started = load_weight(refs, *out_plan, (t, g), out_w, out_sems)
    in_started = load_weight(refs, *in_plan, (t, g), in_w, in_sems)
    for copy in out_started:
        copy.wait()
    tile = 256
    total = mixed.shape[0]
    for b in range(total // tile):
        here = pl.ds(b * tile, tile)
        x = mixed[here]
        for side in (0, 1):
            lanes = pl.ds(side * half, half)
            attended = jnp.dot(x, out_w[side], preferred_element_type=f32)
            middle[here, lanes] = (stream[here, lanes].astype(f32) + attended).astype(bf16)
    for copy in in_started:
        copy.wait()
    for b in range(total // tile):
        here = pl.ds(b * tile, tile)
        x = layer_norm(middle[here].astype(f32), gain[...]).astype(bf16)
        value = jnp.dot(x, in_w[0], preferred_element_type=f32)
        gate = jnp.dot(x, in_w[1], preferred_element_type=f32)
        gated[here] = (value * jax.nn.sigmoid(gate)).astype(bf16)
    for s in range(total // frames):
        edge[pl.ds(s * EDGE, EDGE)] = gated[pl.ds((s + 1) * frames - EDGE, EDGE)]


def conv_kernel(plan, frames, place_ref, gated, edge, middle, starts, taps, gain, *rest):
    count = len(rest) - 6
    refs = rest[:count]
    out, weight, padded, depth, elapsed, sems = rest[count:]
    t, g = place_ref[0], place_ref[1]
    half = weight.shape[2]
    started = load_weight(refs, *plan, (t, g), weight, sems)
    streams = gated.shape[0] // frames
    channels = gated.shape[1]
    lane_tiles = channels // 128
    block = 64
    blocks = frames // block
    for s in range(streams):
        for c in range(lane_tiles):
            lanes = pl.ds(c * 128, 128)
            padded[s * lane_tiles + c, pl.ds(0, EDGE)] = edge[pl.ds(s * EDGE, EDGE), lanes].astype(f32)
            padded[s * lane_tiles + c, pl.ds(EDGE, frames)] = gated[pl.ds(s * frames, frames), lanes].astype(f32)
    row = lax.broadcasted_iota(jnp.int32, (frames, 128), 0) + t * frames
    for s in range(streams):
        elapsed[pl.ds(s * frames, frames)] = row - jnp.broadcast_to(starts[pl.ds(s * frames, frames)], (frames, 128))

    for s in range(streams):

        def body(b, carry, s=s):
            r0 = pl.multiple_of(b * block, block)
            age = elapsed[pl.ds(s * frames + r0, block)]
            for c in range(lane_tiles):
                lanes = pl.ds(c * 128, 128)
                acc = jnp.zeros((block, 128), f32)
                for delay in range(KERNEL):
                    x = padded[s * lane_tiles + c, pl.ds(r0 + EDGE - delay, block)]
                    term = x * taps[pl.ds(KERNEL - 1 - delay, 1), lanes]
                    acc = acc + jnp.where(age >= delay, term, 0.0)
                depth[pl.ds(s * frames + r0, block), lanes] = acc
            return carry

        lax.fori_loop(0, blocks, body, 0)
    for copy in started:
        copy.wait()
    tile = 256
    for b in range(streams * frames // tile):
        here = pl.ds(b * tile, tile)
        n = layer_norm(depth[here], gain[...])
        swished = (n * jax.nn.sigmoid(n)).astype(bf16)
        for side in (0, 1):
            lanes = pl.ds(side * half, half)
            added = jnp.dot(swished, weight[side], preferred_element_type=f32)
            out[here, lanes] = (middle[here, lanes].astype(f32) + added).astype(bf16)


def dma_sems(count):
    return pltpu.SemaphoreType.DMA((count,))


def shards(
    slot_frames,
    slot_live,
    utterance_start,
    in_projection,
    out_projection,
    pointwise_in,
    depthwise,
    pointwise_out,
    gain_attention,
    gain_convolution,
    gain_depth,
):
    devices = lax.axis_size("tm")
    t = lax.axis_index("tm")
    g = lax.axis_index("groups")
    slots, block_rows, width = slot_frames.shape
    owner_blocks = slots // 2
    frames = 2 * block_rows
    streams = owner_blocks // 2
    rows = streams * frames
    part = width // 2
    core = t % 2
    in_half = in_projection.shape[1] // 2
    channels = H * HD
    conv_channels = pointwise_in.shape[1] // 2
    place = jnp.stack([t, g]).astype(jnp.int32)
    every = range(devices)
    across_core = [(i, i ^ 1) for i in every]
    across_x = [(i, i ^ 2) for i in every]
    onward = [(i, i - 4 if i & 2 else i + 4) for i in every]
    onward = [(i, j) for i, j in onward if 0 <= j < devices]
    next_door = [(i, i + 1) for i in range(devices - 1)]
    staged = devices == 16

    def like(shape, dtype=bf16):
        return jax.ShapeDtypeStruct(shape, dtype)

    def to_core(x):
        return lax.ppermute(x, "tm", across_core)

    def to_x(x):
        return lax.ppermute(x, "tm", across_x)

    def to_y(x):
        return lax.ppermute(x, "groups", [(0, 1), (1, 0)])

    def up(x, k):
        return lax.ppermute(x, "tm", [(i, (i + 4 * k) % devices) for i in every])

    def gathered_halves(w):
        full = lax.all_gather(w, "tm", axis=0, tiled=True)
        middle = full.shape[1] // 2
        return jnp.stack([full[:, :middle], full[:, middle:]])

    r_in, r_out, r_expand, r_last = (w.shape[0] for w in (in_projection, out_projection, pointwise_in, pointwise_out))
    r_rest = r_out + r_expand + r_last
    r_first = r_in + r_in // 2
    if staged:
        *half_packs, in_whole = pl.pallas_call(
            prepare_kernel,
            out_shape=[like((r_first, part)), like((r_rest, part)), like((2, r_first, part))],
            in_specs=[SMEM] + [ANY] * 4,
            out_specs=[VMEM] * 3,
            scratch_shapes=[dma_sems(18)],
            compiler_params=params(),
            name="prepare",
        )(place, in_projection, out_projection, pointwise_in, pointwise_out)
        half_in, half_rest = half_packs

    theirs = pl.pallas_call(
        hand_over_kernel,
        out_shape=like((slots, block_rows, part)),
        in_specs=[SMEM, ANY],
        out_specs=VMEM,
        scratch_shapes=[pltpu.SemaphoreType.DMA],
        compiler_params=params(),
        name="hand_over",
    )(place, slot_frames)
    theirs = to_core(theirs)

    live_all = lax.dynamic_update_slice(jnp.zeros((devices * slots,), jnp.int32), slot_live, (t * slots,))
    if staged:
        live_all = after(live_all, half_in)
    live_all = lax.psum(live_all, "tm")
    if staged:
        in_z = [up(after(half_in, live_all), k) for k in (1, 2, 3)]
        in_x = to_x(after(half_in, live_all))
        live_all = after(live_all, in_x)

    per_chunk = slots // CHUNKS
    *leaving, table = pl.pallas_call(
        lambda *r: route_kernel(slots, devices // 2, per_chunk, *r),
        out_shape=[like((per_chunk, block_rows, part))] * CHUNKS + [like((slots,), jnp.int32)],
        in_specs=[SMEM, SMEM, ANY, ANY],
        out_specs=[VMEM] * CHUNKS + [SMEM],
        scratch_shapes=[pltpu.SMEM((slots,), jnp.int32), dma_sems(slots)],
        compiler_params=params(),
        name="route",
    )(place, live_all, slot_frames, theirs)
    beside = [to_x(a) for a in leaving]
    beyond = [lax.ppermute(a, "tm", onward) for a in beside]

    if staged:
        in_column = jnp.stack(after(in_z, beside[0]))
        in_first = jnp.concatenate([in_column, in_x[None]])
        in_third = to_y(in_first)
        in_second = to_x(in_column)
        in_fourth = to_y(in_second)
        rest_mine = lax.all_gather(half_rest, "tm", axis=0, tiled=False)
        quarter = part // 2
        ready = after(rest_mine, *beyond)
        rest_over = []
        for low, high in ((0, r_out + r_expand), (r_out + r_expand, r_rest)):
            sent = lax.dynamic_slice(ready, (0, low, core * quarter), (devices, high - low, quarter))
            rest_over.append(to_y(sent))
        in_arrays = [in_whole, in_first, in_second, in_third, in_fourth]
        in_arrays += [to_core(a) for a in in_arrays]
        over = in_half - part
        half_rows = r_in // 2
        in_segments = [
            (0, r_in, 0, part, 0, 0),
            (r_in, half_rows, 0, over, 0, part),
            (r_in, half_rows, over, over, half_rows, part),
        ]
        in_plan = (piece_copies(), in_segments, r_in)
        pieces = rest_pieces(devices)
        plans = [
            (pieces, [(0, r_out, 0, None, 0, 0)], r_out),
            (pieces, [(r_out, r_expand, 0, None, 0, 0)], r_expand),
            (rest_pieces(devices, r_out + r_expand), [(0, r_last, 0, None, 0, 0)], r_last),
        ]
    else:
        in_arrays = [gathered_halves(in_projection)]
        rest_arrays = [gathered_halves(w) for w in (out_projection, pointwise_in, pointwise_out)]
        in_plan = (whole_weight(0), [(0, width, 0, in_half, 0, 0)], width)
        plans = [
            (whole_weight(i), [(0, count, 0, part, 0, 0)], count)
            for i, count in enumerate((channels, width, conv_channels))
        ]

    keep, give = pl.pallas_call(
        lambda *r: assemble_kernel(slots, per_chunk, *r),
        out_shape=[like((owner_blocks, block_rows, part))] * 2,
        in_specs=[SMEM, SMEM] + [ANY] * (2 + 2 * CHUNKS),
        out_specs=[VMEM] * 2,
        scratch_shapes=[dma_sems(slots)],
        compiler_params=params(),
        name="assemble",
    )(place, table, slot_frames, theirs, *beside, *beyond)
    other = to_core(give)

    stream, q, kv = pl.pallas_call(
        lambda *r: qkv_kernel(*in_plan, *r),
        out_shape=[like((rows, width)), like((rows, channels)), like((2, rows, channels))],
        in_specs=[SMEM, VMEM, VMEM, VMEM] + [ANY] * len(in_arrays),
        out_specs=[VMEM] * 3,
        scratch_shapes=[
            pltpu.VMEM((2, width, in_half), bf16),
            pltpu.VMEM((rows, width), bf16),
            dma_sems(len(in_plan[0]) * len(in_plan[1])),
        ],
        compiler_params=params(),
        name="qkv",
    )(place, keep, other, gain_attention[None], *in_arrays)

    prior = lax.ppermute(kv, "tm", next_door)
    starts = utterance_start.reshape(rows, 1)

    mixed = pl.pallas_call(
        lambda *r: attention_kernel(frames, *r),
        out_shape=like((rows, channels)),
        in_specs=[SMEM] + [VMEM] * 4,
        out_specs=VMEM,
        scratch_shapes=[pltpu.VMEM((2 * rows, channels), bf16)] * 2,
        compiler_params=params(),
        name="attention",
    )(place, q, kv, prior, starts)

    if staged:
        mid_arrays = [rest_mine, rest_over[0], to_core(after(rest_over[0], mixed))]
    else:
        mid_arrays = last_arrays = rest_arrays

    middle, gated, edge = pl.pallas_call(
        lambda *r: gate_kernel(plans[0], plans[1], frames, *r),
        out_shape=[like((rows, width)), like((rows, conv_channels)), like((streams * EDGE, conv_channels))],
        in_specs=[SMEM, VMEM, VMEM, VMEM] + [ANY] * len(mid_arrays),
        out_specs=[VMEM] * 3,
        scratch_shapes=[
            pltpu.VMEM((2, channels, part), bf16),
            pltpu.VMEM((2, width, part), bf16),
            dma_sems(len(plans[0][0])),
            dma_sems(len(plans[1][0])),
        ],
        compiler_params=params(),
        name="gate",
    )(place, mixed, stream, gain_convolution[None], *mid_arrays)
    edge = lax.ppermute(edge, "tm", next_door)
    if staged:
        last_arrays = [rest_mine, rest_over[1], to_core(after(rest_over[1], gated))]

    lane_tiles = conv_channels // 128
    out = pl.pallas_call(
        lambda *r: conv_kernel(plans[2], frames, *r),
        out_shape=like((rows, width)),
        in_specs=[SMEM] + [VMEM] * 6 + [ANY] * len(last_arrays),
        out_specs=VMEM,
        scratch_shapes=[
            pltpu.VMEM((2, conv_channels, part), bf16),
            pltpu.VMEM((streams * lane_tiles, EDGE + frames, 128), f32),
            pltpu.VMEM((rows, conv_channels), f32),
            pltpu.VMEM((rows, 128), jnp.int32),
            dma_sems(len(plans[2][0])),
        ],
        compiler_params=params(),
        name="conv",
    )(place, gated, edge, middle, starts, depthwise, gain_depth[None], *last_arrays)
    return out.reshape(streams, frames, width)


def solution(mesh):
    in_specs = (
        P(("groups", "tm"), None, None),
        P(("groups", "tm")),
        P("groups", "tm"),
        P("tm", None),
        P("tm", None),
        P("tm", None),
        P(),
        P("tm", None),
        P(),
        P(),
        P(),
    )
    out_specs = P("groups", "tm", None)
    return jax.shard_map(shards, mesh=mesh, in_specs=in_specs, out_specs=out_specs, check_vma=False)
```

```python
import math

import jax
import jax.numpy as jnp
from jax import lax
from jax.experimental import pallas as pl
from jax.experimental.pallas import tpu as pltpu
from jax.sharding import PartitionSpec as P

H = 8
HD = 96
KERNEL = 31
CTX = 256
CHUNKS = 2
EDGE = 32
VMEM_LIMIT = 56 << 20

epsilon = 1e-05
bf16 = jnp.bfloat16
f32 = jnp.float32

ANY = pl.BlockSpec(memory_space=pl.ANY)
SMEM = pl.BlockSpec(memory_space=pltpu.SMEM)
VMEM = pl.BlockSpec(memory_space=pltpu.VMEM)


def layer_norm(values, gain_row):
    center = values - jnp.mean(values, axis=-1, keepdims=True)
    spread = jnp.mean(center * center, axis=-1, keepdims=True)
    return center * lax.rsqrt(spread + epsilon) * gain_row


def params():
    return pltpu.CompilerParams(vmem_limit_bytes=VMEM_LIMIT)


def after(value, *earlier):
    return lax.optimization_barrier((value, *earlier))[0]


def whole_weight(index):
    return [(index, side, lambda t: 0, lambda g, side=side: side) for side in (0, 1)]


def piece_copies():
    copies = []
    for flip, base in ((0, 0), (1, 5)):
        for side in (0, 1):
            copies.append((base, side, lambda t, f=flip: t ^ f, lambda g, s=side: s))
        for k in (1, 2, 3):
            plain = lambda t, k=k, f=flip: ((t - 4 * k) & 15) ^ f
            crossed = lambda t, k=k, f=flip: ((t - 4 * k) & 15) ^ (2 + f)
            copies.append((base + 1, k - 1, plain, lambda g: g))
            copies.append((base + 2, k - 1, crossed, lambda g: g))
            copies.append((base + 3, k - 1, plain, lambda g: 1 - g))
            copies.append((base + 4, k - 1, crossed, lambda g: 1 - g))
        next_door = lambda t, f=flip: t ^ (2 + f)
        copies.append((base + 1, 3, next_door, lambda g: g))
        copies.append((base + 3, 3, next_door, lambda g: 1 - g))
    return copies


def rest_pieces(parts, shift=0):
    pieces = []
    for part in range(parts):
        block = lambda t, part=part: part
        pieces.append((0, part, block, lambda g: g, lambda t: 0, shift))
        pieces.append((1, part, block, lambda g: 1 - g, lambda t: t & 1, 0))
        pieces.append((2, part, block, lambda g: 1 - g, lambda t: 1 - (t & 1), 0))
    return pieces


def load_weight(refs, pieces, segments, rows, place, target, sems):
    t, g = place
    started = []
    for array, lead, block, side, *quarter in pieces:
        for row, count, column, columns, row_offset, column_offset in segments:
            source = refs[array].at[lead]
            row = row + quarter[1] if quarter else row
            columns = source.shape[1] if columns is None else columns
            source = source.at[pl.ds(row, count), pl.ds(column, columns)]
            first = block(t)
            first = first * rows if isinstance(first, int) else pl.multiple_of(first * rows, rows)
            if quarter:
                column_offset = quarter[0](t)
                if not isinstance(column_offset, int):
                    column_offset = pl.multiple_of(column_offset * columns, 128)
            spot = target.at[side(g), pl.ds(first + row_offset, count), pl.ds(column_offset, columns)]
            copy = pltpu.make_async_copy(source, spot, sems.at[len(started)])
            copy.start()
            started.append(copy)
    return started


def prepare_kernel(place_ref, w_in, w_out, w_expand, w_last, half, half_rest, whole, sems):
    g = place_ref[1]
    width = half.shape[1]
    rows, columns = w_in.shape
    columns = columns // 2
    over = columns - width
    copies = []
    for target, side in ((half, g), (whole.at[0], 0), (whole.at[1], 1)):

        def lanes(base, size, side=side):
            return pl.ds(base if isinstance(side, int) else pl.multiple_of(base, 128), size)

        copies.append((w_in.at[:, lanes(side * columns, width)], target.at[pl.ds(0, rows)]))
        for part in (0, 1):
            source = w_in.at[pl.ds(part * rows // 2, rows // 2), lanes(side * columns + width, over)]
            copies.append((source, target.at[pl.ds(rows, rows // 2), pl.ds(part * over, over)]))
    row = 0
    for source in (w_out, w_expand, w_last):
        count = source.shape[0]
        copies.append((source.at[:, pl.ds(pl.multiple_of(g * width, 128), width)], half_rest.at[pl.ds(row, count)]))
        row += count
    started = [pltpu.make_async_copy(a, b, sems.at[i]) for i, (a, b) in enumerate(copies)]
    for copy in started:
        copy.start()
    for copy in started:
        copy.wait()


def hand_over_kernel(place_ref, frames, theirs, sem):
    part = theirs.shape[2]
    column = pl.multiple_of((1 - (place_ref[0] & 1)) * part, 128)
    copy = pltpu.make_async_copy(frames.at[:, :, pl.ds(column, part)], theirs, sem)
    copy.start()
    copy.wait()


def route_kernel(slots, chips, per_chunk, place_ref, live_ref, frames, theirs, *rest):
    chunks = rest[:CHUNKS]
    table_ref, leave_ref, sems = rest[CHUNKS:]
    t = place_ref[0]
    core = t & 1
    chip = t >> 1
    chip_slots = 2 * slots
    count = chip_slots // 2
    part = theirs.shape[2]
    mine = frames.at[:, :, pl.ds(pl.multiple_of(core * part, 128), part)]

    for j in range(count):
        table_ref[j] = 0
        leave_ref[j] = 0
    first = jnp.maximum(chip - 1, 0)
    total = lax.fori_loop(0, first * chip_slots, lambda f, s: s + live_ref[f], jnp.int32(0))

    for step in (-1, 0, 1):
        here = chip + step
        inside = (here >= 0) & (here < chips)
        start = jnp.clip(here, 0, chips - 1) * chip_slots
        if step == 0:
            offset = jnp.int32(0)
        else:
            offset = jnp.where(here == (chip ^ 1), chip_slots, chip_slots + count)

        def one(s, carry, step=step, here=here, inside=inside, start=start, offset=offset):
            counted, rank = carry
            live = jnp.where(inside, live_ref[start + s], 0)
            owner = counted // count
            leaving = jnp.where((live > 0) & (owner != here), 1, 0)

            @pl.when((live > 0) & (owner == chip))
            def _():
                table_ref[counted & (count - 1)] = (s if step == 0 else rank & (count - 1)) + offset

            if step == 0:

                @pl.when(leaving > 0)
                def _():
                    leave_ref[rank & (count - 1)] = s

            return counted + live, rank + leaving

        total, _ = lax.fori_loop(0, chip_slots, one, (total, jnp.int32(0)))
    for j in range(count):
        s = leave_ref[j]
        spot = chunks[j // per_chunk].at[j % per_chunk]
        own = (s // slots) == core

        @pl.when(own)
        def _():
            pltpu.make_async_copy(mine.at[s & (slots - 1)], spot, sems.at[j]).start()

        @pl.when(jnp.logical_not(own))
        def _():
            pltpu.make_async_copy(theirs.at[s & (slots - 1)], spot, sems.at[j]).start()

    for j in range(count):
        spot = chunks[j // per_chunk].at[j % per_chunk]
        pltpu.make_async_copy(mine.at[0], spot, sems.at[j]).wait()


def assemble_kernel(slots, per_chunk, place_ref, table_ref, frames, theirs, *rest):
    beside = rest[:CHUNKS]
    beyond = rest[CHUNKS : 2 * CHUNKS]
    keep, give, sems = rest[2 * CHUNKS :]
    core = place_ref[0] & 1
    part = theirs.shape[2]
    mine = frames.at[:, :, pl.ds(pl.multiple_of(core * part, 128), part)]
    count = slots
    blocks = count // 2
    for j in range(blocks):
        for side in (0, 1):
            target = (keep if side == 0 else give).at[j]
            sem = sems.at[side * blocks + j]
            code = table_ref[j + blocks * (core if side == 0 else 1 - core)]
            low = code & (slots - 1)
            local = code < 2 * slots
            own = (code // slots) == core

            @pl.when(local & own)
            def _():
                pltpu.make_async_copy(mine.at[low], target, sem).start()

            @pl.when(local & jnp.logical_not(own))
            def _():
                pltpu.make_async_copy(theirs.at[low], target, sem).start()

            for chunk in range(CHUNKS):
                for which, source in ((0, beside[chunk]), (1, beyond[chunk])):
                    low_end = 2 * slots + which * count + chunk * per_chunk

                    @pl.when((code >= low_end) & (code < low_end + per_chunk))
                    def _():
                        pltpu.make_async_copy(source.at[low & (per_chunk - 1)], target, sem).start()

    for j in range(blocks):
        pltpu.make_async_copy(mine.at[0], keep.at[j], sems.at[j]).wait()
        pltpu.make_async_copy(mine.at[0], give.at[j], sems.at[blocks + j]).wait()


def qkv_kernel(copies, segments, rows, place_ref, keep, other, gain, *rest):
    count = len(rest) - 6
    refs = rest[:count]
    stream, q, kv, weight, normed, sems = rest[count:]
    k, v = kv.at[0], kv.at[1]
    t, g = place_ref[0], place_ref[1]
    core = t & 1
    half = weight.shape[2]
    started = load_weight(refs, copies, segments, rows, (t, g), weight, sems)
    blocks, block_rows, part = keep.shape
    for b in range(blocks):
        a, o = keep[b], other[b]
        low = jnp.where(core == 0, a, o)
        high = jnp.where(core == 0, o, a)
        here = pl.ds(b * block_rows, block_rows)
        stream[here, pl.ds(0, part)] = low
        stream[here, pl.ds(part, part)] = high
        x = jnp.concatenate([low, high], axis=-1).astype(f32)
        normed[here] = layer_norm(x, gain[...]).astype(bf16)
    for copy in started:
        copy.wait()
    width = H * HD
    over = half - width
    tile = 256
    for b in range(blocks * block_rows // tile):
        here = pl.ds(b * tile, tile)
        x = normed[here]
        left = jnp.dot(x, weight[0], preferred_element_type=f32).astype(bf16)
        q[here] = left[:, :width]
        k[here, pl.ds(0, over)] = left[:, width:]
        right = jnp.dot(x, weight[1], preferred_element_type=f32).astype(bf16)
        k[here, pl.ds(over, width - over)] = right[:, : width - over]
        v[here] = right[:, width - over :]


def attention_kernel(frames, place_ref, q, kv, prior, starts, mixed, keys, values):
    k, v, prior_k, prior_v = kv.at[0], kv.at[1], prior.at[0], prior.at[1]
    t = place_ref[0]
    streams = q.shape[0] // frames
    tile = 256
    window = tile + CTX
    for s in range(streams):
        keys[pl.ds(2 * s * frames, frames)] = prior_k[pl.ds(s * frames, frames)]
        keys[pl.ds((2 * s + 1) * frames, frames)] = k[pl.ds(s * frames, frames)]
        values[pl.ds(2 * s * frames, frames)] = prior_v[pl.ds(s * frames, frames)]
        values[pl.ds((2 * s + 1) * frames, frames)] = v[pl.ds(s * frames, frames)]
    scale = 1.0 / math.sqrt(HD) / math.log(2.0)
    tiles = frames // tile

    def body(step, carry):
        s = step // tiles
        part = step % tiles
        here = pl.ds(pl.multiple_of(step * tile, tile), tile)
        there = pl.ds(pl.multiple_of(s * 2 * frames + part * tile, tile), window)
        row = lax.broadcasted_iota(jnp.int32, (tile, window), 0)
        col = lax.broadcasted_iota(jnp.int32, (tile, window), 1)
        begin = starts[here] - (t - 1) * frames - part * tile
        bias = jnp.where((col <= row + CTX) & (col >= row) & (col >= begin), 0.0, -1e30).astype(f32)
        for group in range(H // 4):
            outs = []
            for head in range(4):
                lane0 = head * HD
                first = lane0 // 128 * 128
                last = -(-(lane0 + HD) // 128) * 128
                lanes = pl.ds(group * 4 * HD + first, last - first)
                qs = q[here, lanes]
                lane = lax.broadcasted_iota(jnp.int32, qs.shape, 1) + first
                qs = jnp.where((lane >= lane0) & (lane < lane0 + HD), qs, jnp.zeros_like(qs))
                scores = lax.dot_general(
                    qs, keys[there, lanes], (((1,), (1,)), ((), ())), preferred_element_type=f32
                )
                scores = scores * scale + bias
                raised = jnp.exp2(scores - jnp.max(scores, axis=-1, keepdims=True))
                total = jnp.sum(raised, axis=-1, keepdims=True)
                out = jnp.dot(raised.astype(bf16), values[there, lanes], preferred_element_type=f32)
                outs.append(out * (1.0 / total))
            lane = lax.broadcasted_iota(jnp.int32, (tile, 128), 1)
            base = group * 4 * HD
            mixed[here, pl.ds(base, 128)] = jnp.where(lane < 96, outs[0], outs[1][:, :128]).astype(bf16)
            mixed[here, pl.ds(base + 128, 128)] = jnp.where(lane < 64, outs[1][:, 128:], outs[2][:, :128]).astype(
                bf16
            )
            mixed[here, pl.ds(base + 256, 128)] = jnp.where(lane < 32, outs[2][:, 128:], outs[3]).astype(bf16)
        return carry

    lax.fori_loop(0, streams * tiles, body, 0)


def gate_kernel(out_plan, in_plan, frames, place_ref, mixed, stream, gain, *rest):
    count = len(rest) - 7
    refs = rest[:count]
    middle, gated, edge, out_w, in_w, out_sems, in_sems = rest[count:]
    t, g = place_ref[0], place_ref[1]
    half = out_w.shape[2]
    out_started = load_weight(refs, *out_plan, (t, g), out_w, out_sems)
    in_started = load_weight(refs, *in_plan, (t, g), in_w, in_sems)
    for copy in out_started:
        copy.wait()
    tile = 256
    total = mixed.shape[0]
    for b in range(total // tile):
        here = pl.ds(b * tile, tile)
        x = mixed[here]
        for side in (0, 1):
            lanes = pl.ds(side * half, half)
            attended = jnp.dot(x, out_w[side], preferred_element_type=f32)
            middle[here, lanes] = (stream[here, lanes].astype(f32) + attended).astype(bf16)
    for copy in in_started:
        copy.wait()
    for b in range(total // tile):
        here = pl.ds(b * tile, tile)
        x = layer_norm(middle[here].astype(f32), gain[...]).astype(bf16)
        value = jnp.dot(x, in_w[0], preferred_element_type=f32)
        gate = jnp.dot(x, in_w[1], preferred_element_type=f32)
        gated[here] = (value * jax.nn.sigmoid(gate)).astype(bf16)
    for s in range(total // frames):
        edge[pl.ds(s * EDGE, EDGE)] = gated[pl.ds((s + 1) * frames - EDGE, EDGE)]


def conv_kernel(plan, frames, place_ref, gated, edge, middle, starts, taps, gain, *rest):
    count = len(rest) - 6
    refs = rest[:count]
    out, weight, padded, depth, elapsed, sems = rest[count:]
    t, g = place_ref[0], place_ref[1]
    half = weight.shape[2]
    started = load_weight(refs, *plan, (t, g), weight, sems)
    streams = gated.shape[0] // frames
    channels = gated.shape[1]
    lane_tiles = channels // 128
    block = 64
    blocks = frames // block
    for s in range(streams):
        for c in range(lane_tiles):
            lanes = pl.ds(c * 128, 128)
            padded[s * lane_tiles + c, pl.ds(0, EDGE)] = edge[pl.ds(s * EDGE, EDGE), lanes].astype(f32)
            padded[s * lane_tiles + c, pl.ds(EDGE, frames)] = gated[pl.ds(s * frames, frames), lanes].astype(f32)
    row = lax.broadcasted_iota(jnp.int32, (frames, 128), 0) + t * frames
    for s in range(streams):
        elapsed[pl.ds(s * frames, frames)] = row - jnp.broadcast_to(starts[pl.ds(s * frames, frames)], (frames, 128))

    for s in range(streams):

        def body(b, carry, s=s):
            r0 = pl.multiple_of(b * block, block)
            age = elapsed[pl.ds(s * frames + r0, block)]
            for c in range(lane_tiles):
                lanes = pl.ds(c * 128, 128)
                acc = jnp.zeros((block, 128), f32)
                for delay in range(KERNEL):
                    x = padded[s * lane_tiles + c, pl.ds(r0 + EDGE - delay, block)]
                    term = x * taps[pl.ds(KERNEL - 1 - delay, 1), lanes]
                    acc = acc + jnp.where(age >= delay, term, 0.0)
                depth[pl.ds(s * frames + r0, block), lanes] = acc
            return carry

        lax.fori_loop(0, blocks, body, 0)
    for copy in started:
        copy.wait()
    tile = 256
    for b in range(streams * frames // tile):
        here = pl.ds(b * tile, tile)
        n = layer_norm(depth[here], gain[...])
        swished = (n * jax.nn.sigmoid(n)).astype(bf16)
        for side in (0, 1):
            lanes = pl.ds(side * half, half)
            added = jnp.dot(swished, weight[side], preferred_element_type=f32)
            out[here, lanes] = (middle[here, lanes].astype(f32) + added).astype(bf16)


def dma_sems(count):
    return pltpu.SemaphoreType.DMA((count,))


def shards(
    slot_frames,
    slot_live,
    utterance_start,
    in_projection,
    out_projection,
    pointwise_in,
    depthwise,
    pointwise_out,
    gain_attention,
    gain_convolution,
    gain_depth,
):
    devices = lax.axis_size("tm")
    t = lax.axis_index("tm")
    g = lax.axis_index("groups")
    slots, block_rows, width = slot_frames.shape
    owner_blocks = slots // 2
    frames = 2 * block_rows
    streams = owner_blocks // 2
    rows = streams * frames
    part = width // 2
    core = t % 2
    in_half = in_projection.shape[1] // 2
    channels = H * HD
    conv_channels = pointwise_in.shape[1] // 2
    place = jnp.stack([t, g]).astype(jnp.int32)
    every = range(devices)
    across_core = [(i, i ^ 1) for i in every]
    across_x = [(i, i ^ 2) for i in every]
    onward = [(i, i - 4 if i & 2 else i + 4) for i in every]
    onward = [(i, j) for i, j in onward if 0 <= j < devices]
    next_door = [(i, i + 1) for i in range(devices - 1)]
    staged = devices == 16

    def like(shape, dtype=bf16):
        return jax.ShapeDtypeStruct(shape, dtype)

    def to_core(x):
        return lax.ppermute(x, "tm", across_core)

    def to_x(x):
        return lax.ppermute(x, "tm", across_x)

    def to_y(x):
        return lax.ppermute(x, "groups", [(0, 1), (1, 0)])

    def up(x, k):
        return lax.ppermute(x, "tm", [(i, (i + 4 * k) % devices) for i in every])

    def gathered_halves(w):
        full = lax.all_gather(w, "tm", axis=0, tiled=True)
        middle = full.shape[1] // 2
        return jnp.stack([full[:, :middle], full[:, middle:]])

    r_in, r_out, r_expand, r_last = (w.shape[0] for w in (in_projection, out_projection, pointwise_in, pointwise_out))
    r_rest = r_out + r_expand + r_last
    r_first = r_in + r_in // 2
    if staged:
        *half_packs, in_whole = pl.pallas_call(
            prepare_kernel,
            out_shape=[like((r_first, part)), like((r_rest, part)), like((2, r_first, part))],
            in_specs=[SMEM] + [ANY] * 4,
            out_specs=[VMEM] * 3,
            scratch_shapes=[dma_sems(18)],
            compiler_params=params(),
            name="prepare",
        )(place, in_projection, out_projection, pointwise_in, pointwise_out)
        half_in, half_rest = half_packs

    theirs = pl.pallas_call(
        hand_over_kernel,
        out_shape=like((slots, block_rows, part)),
        in_specs=[SMEM, ANY],
        out_specs=VMEM,
        scratch_shapes=[pltpu.SemaphoreType.DMA],
        compiler_params=params(),
        name="hand_over",
    )(place, slot_frames)
    theirs = to_core(theirs)

    live_all = lax.dynamic_update_slice(jnp.zeros((devices * slots,), jnp.int32), slot_live, (t * slots,))
    if staged:
        live_all = after(live_all, half_in)
    live_all = lax.psum(live_all, "tm")
    if staged:
        in_z = [up(after(half_in, live_all), k) for k in (1, 2, 3)]
        in_x = to_x(after(half_in, live_all))
        live_all = after(live_all, in_x)

    per_chunk = slots // CHUNKS
    *leaving, table = pl.pallas_call(
        lambda *r: route_kernel(slots, devices // 2, per_chunk, *r),
        out_shape=[like((per_chunk, block_rows, part))] * CHUNKS + [like((slots,), jnp.int32)],
        in_specs=[SMEM, SMEM, ANY, ANY],
        out_specs=[VMEM] * CHUNKS + [SMEM],
        scratch_shapes=[pltpu.SMEM((slots,), jnp.int32), dma_sems(slots)],
        compiler_params=params(),
        name="route",
    )(place, live_all, slot_frames, theirs)
    beside = [to_x(a) for a in leaving]
    beyond = [lax.ppermute(a, "tm", onward) for a in beside]

    if staged:
        in_column = jnp.stack(after(in_z, beside[0]))
        in_first = jnp.concatenate([in_column, in_x[None]])
        in_third = to_y(in_first)
        in_second = to_x(in_column)
        in_fourth = to_y(in_second)
        rest_mine = lax.all_gather(half_rest, "tm", axis=0, tiled=False)
        quarter = part // 2
        ready = after(rest_mine, *beyond)
        rest_over = []
        for low, high in ((0, r_out + r_expand), (r_out + r_expand, r_rest)):
            sent = lax.dynamic_slice(ready, (0, low, core * quarter), (devices, high - low, quarter))
            rest_over.append(to_y(sent))
        in_arrays = [in_whole, in_first, in_second, in_third, in_fourth]
        in_arrays += [to_core(a) for a in in_arrays]
        over = in_half - part
        half_rows = r_in // 2
        in_segments = [
            (0, r_in, 0, part, 0, 0),
            (r_in, half_rows, 0, over, 0, part),
            (r_in, half_rows, over, over, half_rows, part),
        ]
        in_plan = (piece_copies(), in_segments, r_in)
        pieces = rest_pieces(devices)
        plans = [
            (pieces, [(0, r_out, 0, None, 0, 0)], r_out),
            (pieces, [(r_out, r_expand, 0, None, 0, 0)], r_expand),
            (rest_pieces(devices, r_out + r_expand), [(0, r_last, 0, None, 0, 0)], r_last),
        ]
    else:
        in_arrays = [gathered_halves(in_projection)]
        rest_arrays = [gathered_halves(w) for w in (out_projection, pointwise_in, pointwise_out)]
        in_plan = (whole_weight(0), [(0, width, 0, in_half, 0, 0)], width)
        plans = [
            (whole_weight(i), [(0, count, 0, part, 0, 0)], count)
            for i, count in enumerate((channels, width, conv_channels))
        ]

    keep, give = pl.pallas_call(
        lambda *r: assemble_kernel(slots, per_chunk, *r),
        out_shape=[like((owner_blocks, block_rows, part))] * 2,
        in_specs=[SMEM, SMEM] + [ANY] * (2 + 2 * CHUNKS),
        out_specs=[VMEM] * 2,
        scratch_shapes=[dma_sems(slots)],
        compiler_params=params(),
        name="assemble",
    )(place, table, slot_frames, theirs, *beside, *beyond)
    other = to_core(give)

    stream, q, kv = pl.pallas_call(
        lambda *r: qkv_kernel(*in_plan, *r),
        out_shape=[like((rows, width)), like((rows, channels)), like((2, rows, channels))],
        in_specs=[SMEM, VMEM, VMEM, VMEM] + [ANY] * len(in_arrays),
        out_specs=[VMEM] * 3,
        scratch_shapes=[
            pltpu.VMEM((2, width, in_half), bf16),
            pltpu.VMEM((rows, width), bf16),
            dma_sems(len(in_plan[0]) * len(in_plan[1])),
        ],
        compiler_params=params(),
        name="qkv",
    )(place, keep, other, gain_attention[None], *in_arrays)

    prior = lax.ppermute(kv, "tm", next_door)
    starts = utterance_start.reshape(rows, 1)

    mixed = pl.pallas_call(
        lambda *r: attention_kernel(frames, *r),
        out_shape=like((rows, channels)),
        in_specs=[SMEM] + [VMEM] * 4,
        out_specs=VMEM,
        scratch_shapes=[pltpu.VMEM((2 * rows, channels), bf16)] * 2,
        compiler_params=params(),
        name="attention",
    )(place, q, kv, prior, starts)

    if staged:
        mid_arrays = [rest_mine, rest_over[0], to_core(after(rest_over[0], mixed))]
    else:
        mid_arrays = last_arrays = rest_arrays

    middle, gated, edge = pl.pallas_call(
        lambda *r: gate_kernel(plans[0], plans[1], frames, *r),
        out_shape=[like((rows, width)), like((rows, conv_channels)), like((streams * EDGE, conv_channels))],
        in_specs=[SMEM, VMEM, VMEM, VMEM] + [ANY] * len(mid_arrays),
        out_specs=[VMEM] * 3,
        scratch_shapes=[
            pltpu.VMEM((2, channels, part), bf16),
            pltpu.VMEM((2, width, part), bf16),
            dma_sems(len(plans[0][0])),
            dma_sems(len(plans[1][0])),
        ],
        compiler_params=params(),
        name="gate",
    )(place, mixed, stream, gain_convolution[None], *mid_arrays)
    edge = lax.ppermute(edge, "tm", next_door)
    if staged:
        last_arrays = [rest_mine, rest_over[1], to_core(after(rest_over[1], gated))]

    lane_tiles = conv_channels // 128
    out = pl.pallas_call(
        lambda *r: conv_kernel(plans[2], frames, *r),
        out_shape=like((rows, width)),
        in_specs=[SMEM] + [VMEM] * 6 + [ANY] * len(last_arrays),
        out_specs=VMEM,
        scratch_shapes=[
            pltpu.VMEM((2, conv_channels, part), bf16),
            pltpu.VMEM((streams * lane_tiles, EDGE + frames, 128), f32),
            pltpu.VMEM((rows, conv_channels), f32),
            pltpu.VMEM((rows, 128), jnp.int32),
            dma_sems(len(plans[2][0])),
        ],
        compiler_params=params(),
        name="conv",
    )(place, gated, edge, middle, starts, depthwise, gain_depth[None], *last_arrays)
    return out.reshape(streams, frames, width)


def solution(mesh):
    in_specs = (
        P(("groups", "tm"), None, None),
        P(("groups", "tm")),
        P("groups", "tm"),
        P("tm", None),
        P("tm", None),
        P("tm", None),
        P(),
        P("tm", None),
        P(),
        P(),
        P(),
    )
    out_specs = P("groups", "tm", None)
    return jax.shard_map(shards, mesh=mesh, in_specs=in_specs, out_specs=out_specs, check_vma=False)
```

```python
import math

import jax
import jax.numpy as jnp
from jax import lax
from jax.experimental import pallas as pl
from jax.experimental.pallas import tpu as pltpu
from jax.sharding import PartitionSpec as P

H = 8
HD = 96
KERNEL = 31
CTX = 256
CHUNKS = 2
EDGE = 32
VMEM_LIMIT = 56 << 20

epsilon = 1e-05
bf16 = jnp.bfloat16
f32 = jnp.float32

ANY = pl.BlockSpec(memory_space=pl.ANY)
SMEM = pl.BlockSpec(memory_space=pltpu.SMEM)
VMEM = pl.BlockSpec(memory_space=pltpu.VMEM)


def layer_norm(values, gain_row):
    center = values - jnp.mean(values, axis=-1, keepdims=True)
    spread = jnp.mean(center * center, axis=-1, keepdims=True)
    return center * lax.rsqrt(spread + epsilon) * gain_row


def params():
    return pltpu.CompilerParams(vmem_limit_bytes=VMEM_LIMIT)


def after(value, *earlier):
    return lax.optimization_barrier((value, *earlier))[0]


def whole_weight(index):
    return [(index, side, lambda t: 0, lambda g, side=side: side) for side in (0, 1)]


def piece_copies():
    copies = []
    for flip, base in ((0, 0), (1, 5)):
        for side in (0, 1):
            copies.append((base, side, lambda t, f=flip: t ^ f, lambda g, s=side: s))
        for k in (1, 2, 3):
            plain = lambda t, k=k, f=flip: ((t - 4 * k) & 15) ^ f
            crossed = lambda t, k=k, f=flip: ((t - 4 * k) & 15) ^ (2 + f)
            copies.append((base + 1, k - 1, plain, lambda g: g))
            copies.append((base + 2, k - 1, crossed, lambda g: g))
            copies.append((base + 3, k - 1, plain, lambda g: 1 - g))
            copies.append((base + 4, k - 1, crossed, lambda g: 1 - g))
        next_door = lambda t, f=flip: t ^ (2 + f)
        copies.append((base + 1, 3, next_door, lambda g: g))
        copies.append((base + 3, 3, next_door, lambda g: 1 - g))
    return copies


def rest_pieces(parts, shift=0):
    pieces = []
    for part in range(parts):
        block = lambda t, part=part: part
        pieces.append((0, part, block, lambda g: g, lambda t: 0, shift))
        pieces.append((1, part, block, lambda g: 1 - g, lambda t: t & 1, 0))
        pieces.append((2, part, block, lambda g: 1 - g, lambda t: 1 - (t & 1), 0))
    return pieces


def load_weight(refs, pieces, segments, rows, place, target, sems):
    t, g = place
    started = []
    for array, lead, block, side, *quarter in pieces:
        for row, count, column, columns, row_offset, column_offset in segments:
            source = refs[array].at[lead]
            row = row + quarter[1] if quarter else row
            columns = source.shape[1] if columns is None else columns
            source = source.at[pl.ds(row, count), pl.ds(column, columns)]
            first = block(t)
            first = first * rows if isinstance(first, int) else pl.multiple_of(first * rows, rows)
            if quarter:
                column_offset = quarter[0](t)
                if not isinstance(column_offset, int):
                    column_offset = pl.multiple_of(column_offset * columns, 128)
            spot = target.at[side(g), pl.ds(first + row_offset, count), pl.ds(column_offset, columns)]
            copy = pltpu.make_async_copy(source, spot, sems.at[len(started)])
            copy.start()
            started.append(copy)
    return started


def prepare_kernel(place_ref, w_in, w_out, w_expand, w_last, half, half_rest, whole, sems):
    g = place_ref[1]
    width = half.shape[1]
    rows, columns = w_in.shape
    columns = columns // 2
    over = columns - width
    copies = []
    for target, side in ((half, g), (whole.at[0], 0), (whole.at[1], 1)):

        def lanes(base, size, side=side):
            return pl.ds(base if isinstance(side, int) else pl.multiple_of(base, 128), size)

        copies.append((w_in.at[:, lanes(side * columns, width)], target.at[pl.ds(0, rows)]))
        for part in (0, 1):
            source = w_in.at[pl.ds(part * rows // 2, rows // 2), lanes(side * columns + width, over)]
            copies.append((source, target.at[pl.ds(rows, rows // 2), pl.ds(part * over, over)]))
    row = 0
    for source in (w_out, w_expand, w_last):
        count = source.shape[0]
        copies.append((source.at[:, pl.ds(pl.multiple_of(g * width, 128), width)], half_rest.at[pl.ds(row, count)]))
        row += count
    started = [pltpu.make_async_copy(a, b, sems.at[i]) for i, (a, b) in enumerate(copies)]
    for copy in started:
        copy.start()
    for copy in started:
        copy.wait()


def hand_over_kernel(place_ref, frames, theirs, sem):
    part = theirs.shape[2]
    column = pl.multiple_of((1 - (place_ref[0] & 1)) * part, 128)
    copy = pltpu.make_async_copy(frames.at[:, :, pl.ds(column, part)], theirs, sem)
    copy.start()
    copy.wait()


def route_kernel(slots, chips, per_chunk, place_ref, live_ref, frames, theirs, *rest):
    chunks = rest[:CHUNKS]
    table_ref, leave_ref, sems = rest[CHUNKS:]
    t = place_ref[0]
    core = t & 1
    chip = t >> 1
    chip_slots = 2 * slots
    count = chip_slots // 2
    part = theirs.shape[2]
    mine = frames.at[:, :, pl.ds(pl.multiple_of(core * part, 128), part)]

    for j in range(count):
        table_ref[j] = 0
        leave_ref[j] = 0
    first = jnp.maximum(chip - 1, 0)
    total = lax.fori_loop(0, first * chip_slots, lambda f, s: s + live_ref[f], jnp.int32(0))

    for step in (-1, 0, 1):
        here = chip + step
        inside = (here >= 0) & (here < chips)
        start = jnp.clip(here, 0, chips - 1) * chip_slots
        if step == 0:
            offset = jnp.int32(0)
        else:
            offset = jnp.where(here == (chip ^ 1), chip_slots, chip_slots + count)

        def one(s, carry, step=step, here=here, inside=inside, start=start, offset=offset):
            counted, rank = carry
            live = jnp.where(inside, live_ref[start + s], 0)
            owner = counted // count
            leaving = jnp.where((live > 0) & (owner != here), 1, 0)

            @pl.when((live > 0) & (owner == chip))
            def _():
                table_ref[counted & (count - 1)] = (s if step == 0 else rank & (count - 1)) + offset

            if step == 0:

                @pl.when(leaving > 0)
                def _():
                    leave_ref[rank & (count - 1)] = s

            return counted + live, rank + leaving

        total, _ = lax.fori_loop(0, chip_slots, one, (total, jnp.int32(0)))
    for j in range(count):
        s = leave_ref[j]
        spot = chunks[j // per_chunk].at[j % per_chunk]
        own = (s // slots) == core

        @pl.when(own)
        def _():
            pltpu.make_async_copy(mine.at[s & (slots - 1)], spot, sems.at[j]).start()

        @pl.when(jnp.logical_not(own))
        def _():
            pltpu.make_async_copy(theirs.at[s & (slots - 1)], spot, sems.at[j]).start()

    for j in range(count):
        spot = chunks[j // per_chunk].at[j % per_chunk]
        pltpu.make_async_copy(mine.at[0], spot, sems.at[j]).wait()


def assemble_kernel(slots, per_chunk, place_ref, table_ref, frames, theirs, *rest):
    beside = rest[:CHUNKS]
    beyond = rest[CHUNKS : 2 * CHUNKS]
    keep, give, sems = rest[2 * CHUNKS :]
    core = place_ref[0] & 1
    part = theirs.shape[2]
    mine = frames.at[:, :, pl.ds(pl.multiple_of(core * part, 128), part)]
    count = slots
    blocks = count // 2
    for j in range(blocks):
        for side in (0, 1):
            target = (keep if side == 0 else give).at[j]
            sem = sems.at[side * blocks + j]
            code = table_ref[j + blocks * (core if side == 0 else 1 - core)]
            low = code & (slots - 1)
            local = code < 2 * slots
            own = (code // slots) == core

            @pl.when(local & own)
            def _():
                pltpu.make_async_copy(mine.at[low], target, sem).start()

            @pl.when(local & jnp.logical_not(own))
            def _():
                pltpu.make_async_copy(theirs.at[low], target, sem).start()

            for chunk in range(CHUNKS):
                for which, source in ((0, beside[chunk]), (1, beyond[chunk])):
                    low_end = 2 * slots + which * count + chunk * per_chunk

                    @pl.when((code >= low_end) & (code < low_end + per_chunk))
                    def _():
                        pltpu.make_async_copy(source.at[low & (per_chunk - 1)], target, sem).start()

    for j in range(blocks):
        pltpu.make_async_copy(mine.at[0], keep.at[j], sems.at[j]).wait()
        pltpu.make_async_copy(mine.at[0], give.at[j], sems.at[blocks + j]).wait()


def qkv_kernel(copies, segments, rows, place_ref, keep, other, gain, *rest):
    count = len(rest) - 6
    refs = rest[:count]
    stream, q, kv, weight, normed, sems = rest[count:]
    k, v = kv.at[0], kv.at[1]
    t, g = place_ref[0], place_ref[1]
    core = t & 1
    half = weight.shape[2]
    started = load_weight(refs, copies, segments, rows, (t, g), weight, sems)
    blocks, block_rows, part = keep.shape
    for b in range(blocks):
        a, o = keep[b], other[b]
        low = jnp.where(core == 0, a, o)
        high = jnp.where(core == 0, o, a)
        here = pl.ds(b * block_rows, block_rows)
        stream[here, pl.ds(0, part)] = low
        stream[here, pl.ds(part, part)] = high
        x = jnp.concatenate([low, high], axis=-1).astype(f32)
        normed[here] = layer_norm(x, gain[...]).astype(bf16)
    for copy in started:
        copy.wait()
    width = H * HD
    over = half - width
    tile = 256
    for b in range(blocks * block_rows // tile):
        here = pl.ds(b * tile, tile)
        x = normed[here]
        left = jnp.dot(x, weight[0], preferred_element_type=f32).astype(bf16)
        q[here] = left[:, :width]
        k[here, pl.ds(0, over)] = left[:, width:]
        right = jnp.dot(x, weight[1], preferred_element_type=f32).astype(bf16)
        k[here, pl.ds(over, width - over)] = right[:, : width - over]
        v[here] = right[:, width - over :]


def attention_kernel(frames, place_ref, q, kv, prior, starts, mixed, keys, values):
    k, v, prior_k, prior_v = kv.at[0], kv.at[1], prior.at[0], prior.at[1]
    t = place_ref[0]
    streams = q.shape[0] // frames
    tile = 256
    window = tile + CTX
    for s in range(streams):
        keys[pl.ds(2 * s * frames, frames)] = prior_k[pl.ds(s * frames, frames)]
        keys[pl.ds((2 * s + 1) * frames, frames)] = k[pl.ds(s * frames, frames)]
        values[pl.ds(2 * s * frames, frames)] = prior_v[pl.ds(s * frames, frames)]
        values[pl.ds((2 * s + 1) * frames, frames)] = v[pl.ds(s * frames, frames)]
    scale = 1.0 / math.sqrt(HD) / math.log(2.0)
    tiles = frames // tile

    def body(step, carry):
        s = step // tiles
        part = step % tiles
        here = pl.ds(pl.multiple_of(step * tile, tile), tile)
        there = pl.ds(pl.multiple_of(s * 2 * frames + part * tile, tile), window)
        row = lax.broadcasted_iota(jnp.int32, (tile, window), 0)
        col = lax.broadcasted_iota(jnp.int32, (tile, window), 1)
        begin = starts[here] - (t - 1) * frames - part * tile
        bias = jnp.where((col <= row + CTX) & (col >= row) & (col >= begin), 0.0, -1e30).astype(f32)
        for group in range(H // 4):
            outs = []
            for head in range(4):
                lane0 = head * HD
                first = lane0 // 128 * 128
                last = -(-(lane0 + HD) // 128) * 128
                lanes = pl.ds(group * 4 * HD + first, last - first)
                qs = q[here, lanes]
                lane = lax.broadcasted_iota(jnp.int32, qs.shape, 1) + first
                qs = jnp.where((lane >= lane0) & (lane < lane0 + HD), qs, jnp.zeros_like(qs))
                scores = lax.dot_general(
                    qs, keys[there, lanes], (((1,), (1,)), ((), ())), preferred_element_type=f32
                )
                scores = scores * scale + bias
                raised = jnp.exp2(scores - jnp.max(scores, axis=-1, keepdims=True))
                total = jnp.sum(raised, axis=-1, keepdims=True)
                out = jnp.dot(raised.astype(bf16), values[there, lanes], preferred_element_type=f32)
                outs.append(out * (1.0 / total))
            lane = lax.broadcasted_iota(jnp.int32, (tile, 128), 1)
            base = group * 4 * HD
            mixed[here, pl.ds(base, 128)] = jnp.where(lane < 96, outs[0], outs[1][:, :128]).astype(bf16)
            mixed[here, pl.ds(base + 128, 128)] = jnp.where(lane < 64, outs[1][:, 128:], outs[2][:, :128]).astype(
                bf16
            )
            mixed[here, pl.ds(base + 256, 128)] = jnp.where(lane < 32, outs[2][:, 128:], outs[3]).astype(bf16)
        return carry

    lax.fori_loop(0, streams * tiles, body, 0, unroll=True)


def gate_kernel(out_plan, in_plan, frames, place_ref, mixed, stream, gain, *rest):
    count = len(rest) - 7
    refs = rest[:count]
    middle, gated, edge, out_w, in_w, out_sems, in_sems = rest[count:]
    t, g = place_ref[0], place_ref[1]
    half = out_w.shape[2]
    out_started = load_weight(refs, *out_plan, (t, g), out_w, out_sems)
    in_started = load_weight(refs, *in_plan, (t, g), in_w, in_sems)
    for copy in out_started:
        copy.wait()
    tile = 256
    total = mixed.shape[0]
    for b in range(total // tile):
        here = pl.ds(b * tile, tile)
        x = mixed[here]
        for side in (0, 1):
            lanes = pl.ds(side * half, half)
            attended = jnp.dot(x, out_w[side], preferred_element_type=f32)
            middle[here, lanes] = (stream[here, lanes].astype(f32) + attended).astype(bf16)
    for copy in in_started:
        copy.wait()
    for b in range(total // tile):
        here = pl.ds(b * tile, tile)
        x = layer_norm(middle[here].astype(f32), gain[...]).astype(bf16)
        value = jnp.dot(x, in_w[0], preferred_element_type=f32)
        gate = jnp.dot(x, in_w[1], preferred_element_type=f32)
        gated[here] = (value * jax.nn.sigmoid(gate)).astype(bf16)
    for s in range(total // frames):
        edge[pl.ds(s * EDGE, EDGE)] = gated[pl.ds((s + 1) * frames - EDGE, EDGE)]


def conv_kernel(plan, frames, place_ref, gated, edge, middle, starts, taps, gain, *rest):
    count = len(rest) - 6
    refs = rest[:count]
    out, weight, padded, depth, elapsed, sems = rest[count:]
    t, g = place_ref[0], place_ref[1]
    half = weight.shape[2]
    started = load_weight(refs, *plan, (t, g), weight, sems)
    streams = gated.shape[0] // frames
    channels = gated.shape[1]
    lane_tiles = channels // 128
    block = 64
    blocks = frames // block
    for s in range(streams):
        for c in range(lane_tiles):
            lanes = pl.ds(c * 128, 128)
            padded[s * lane_tiles + c, pl.ds(0, EDGE)] = edge[pl.ds(s * EDGE, EDGE), lanes].astype(f32)
            padded[s * lane_tiles + c, pl.ds(EDGE, frames)] = gated[pl.ds(s * frames, frames), lanes].astype(f32)
    row = lax.broadcasted_iota(jnp.int32, (frames, 128), 0) + t * frames
    for s in range(streams):
        elapsed[pl.ds(s * frames, frames)] = row - jnp.broadcast_to(starts[pl.ds(s * frames, frames)], (frames, 128))

    for s in range(streams):

        def body(b, carry, s=s):
            r0 = pl.multiple_of(b * block, block)
            age = elapsed[pl.ds(s * frames + r0, block)]
            for c in range(lane_tiles):
                lanes = pl.ds(c * 128, 128)
                acc = jnp.zeros((block, 128), f32)
                for delay in range(KERNEL):
                    x = padded[s * lane_tiles + c, pl.ds(r0 + EDGE - delay, block)]
                    term = x * taps[pl.ds(KERNEL - 1 - delay, 1), lanes]
                    acc = acc + jnp.where(age >= delay, term, 0.0)
                depth[pl.ds(s * frames + r0, block), lanes] = acc
            return carry

        lax.fori_loop(0, blocks, body, 0)
    for copy in started:
        copy.wait()
    tile = 256
    for b in range(streams * frames // tile):
        here = pl.ds(b * tile, tile)
        n = layer_norm(depth[here], gain[...])
        swished = (n * jax.nn.sigmoid(n)).astype(bf16)
        for side in (0, 1):
            lanes = pl.ds(side * half, half)
            added = jnp.dot(swished, weight[side], preferred_element_type=f32)
            out[here, lanes] = (middle[here, lanes].astype(f32) + added).astype(bf16)


def dma_sems(count):
    return pltpu.SemaphoreType.DMA((count,))


def shards(
    slot_frames,
    slot_live,
    utterance_start,
    in_projection,
    out_projection,
    pointwise_in,
    depthwise,
    pointwise_out,
    gain_attention,
    gain_convolution,
    gain_depth,
):
    devices = lax.axis_size("tm")
    t = lax.axis_index("tm")
    g = lax.axis_index("groups")
    slots, block_rows, width = slot_frames.shape
    owner_blocks = slots // 2
    frames = 2 * block_rows
    streams = owner_blocks // 2
    rows = streams * frames
    part = width // 2
    core = t % 2
    in_half = in_projection.shape[1] // 2
    channels = H * HD
    conv_channels = pointwise_in.shape[1] // 2
    place = jnp.stack([t, g]).astype(jnp.int32)
    every = range(devices)
    across_core = [(i, i ^ 1) for i in every]
    across_x = [(i, i ^ 2) for i in every]
    onward = [(i, i - 4 if i & 2 else i + 4) for i in every]
    onward = [(i, j) for i, j in onward if 0 <= j < devices]
    next_door = [(i, i + 1) for i in range(devices - 1)]
    staged = devices == 16

    def like(shape, dtype=bf16):
        return jax.ShapeDtypeStruct(shape, dtype)

    def to_core(x):
        return lax.ppermute(x, "tm", across_core)

    def to_x(x):
        return lax.ppermute(x, "tm", across_x)

    def to_y(x):
        return lax.ppermute(x, "groups", [(0, 1), (1, 0)])

    def up(x, k):
        return lax.ppermute(x, "tm", [(i, (i + 4 * k) % devices) for i in every])

    def gathered_halves(w):
        full = lax.all_gather(w, "tm", axis=0, tiled=True)
        middle = full.shape[1] // 2
        return jnp.stack([full[:, :middle], full[:, middle:]])

    r_in, r_out, r_expand, r_last = (w.shape[0] for w in (in_projection, out_projection, pointwise_in, pointwise_out))
    r_rest = r_out + r_expand + r_last
    r_first = r_in + r_in // 2
    if staged:
        *half_packs, in_whole = pl.pallas_call(
            prepare_kernel,
            out_shape=[like((r_first, part)), like((r_rest, part)), like((2, r_first, part))],
            in_specs=[SMEM] + [ANY] * 4,
            out_specs=[VMEM] * 3,
            scratch_shapes=[dma_sems(18)],
            compiler_params=params(),
            name="prepare",
        )(place, in_projection, out_projection, pointwise_in, pointwise_out)
        half_in, half_rest = half_packs

    theirs = pl.pallas_call(
        hand_over_kernel,
        out_shape=like((slots, block_rows, part)),
        in_specs=[SMEM, ANY],
        out_specs=VMEM,
        scratch_shapes=[pltpu.SemaphoreType.DMA],
        compiler_params=params(),
        name="hand_over",
    )(place, slot_frames)
    theirs = to_core(theirs)

    live_all = lax.dynamic_update_slice(jnp.zeros((devices * slots,), jnp.int32), slot_live, (t * slots,))
    if staged:
        live_all = after(live_all, half_in)
    live_all = lax.psum(live_all, "tm")
    if staged:
        in_z = [up(after(half_in, live_all), k) for k in (1, 2, 3)]
        in_x = to_x(after(half_in, live_all))
        live_all = after(live_all, in_x)

    per_chunk = slots // CHUNKS
    *leaving, table = pl.pallas_call(
        lambda *r: route_kernel(slots, devices // 2, per_chunk, *r),
        out_shape=[like((per_chunk, block_rows, part))] * CHUNKS + [like((slots,), jnp.int32)],
        in_specs=[SMEM, SMEM, ANY, ANY],
        out_specs=[VMEM] * CHUNKS + [SMEM],
        scratch_shapes=[pltpu.SMEM((slots,), jnp.int32), dma_sems(slots)],
        compiler_params=params(),
        name="route",
    )(place, live_all, slot_frames, theirs)
    beside = [to_x(a) for a in leaving]
    beyond = [lax.ppermute(a, "tm", onward) for a in beside]

    if staged:
        in_column = jnp.stack(after(in_z, beside[0]))
        in_first = jnp.concatenate([in_column, in_x[None]])
        in_third = to_y(in_first)
        in_second = to_x(in_column)
        in_fourth = to_y(in_second)
        rest_mine = lax.all_gather(half_rest, "tm", axis=0, tiled=False)
        quarter = part // 2
        ready = after(rest_mine, *beyond)
        rest_over = []
        for low, high in ((0, r_out + r_expand), (r_out + r_expand, r_rest)):
            sent = lax.dynamic_slice(ready, (0, low, core * quarter), (devices, high - low, quarter))
            rest_over.append(to_y(sent))
        in_arrays = [in_whole, in_first, in_second, in_third, in_fourth]
        in_arrays += [to_core(a) for a in in_arrays]
        over = in_half - part
        half_rows = r_in // 2
        in_segments = [
            (0, r_in, 0, part, 0, 0),
            (r_in, half_rows, 0, over, 0, part),
            (r_in, half_rows, over, over, half_rows, part),
        ]
        in_plan = (piece_copies(), in_segments, r_in)
        pieces = rest_pieces(devices)
        plans = [
            (pieces, [(0, r_out, 0, None, 0, 0)], r_out),
            (pieces, [(r_out, r_expand, 0, None, 0, 0)], r_expand),
            (rest_pieces(devices, r_out + r_expand), [(0, r_last, 0, None, 0, 0)], r_last),
        ]
    else:
        in_arrays = [gathered_halves(in_projection)]
        rest_arrays = [gathered_halves(w) for w in (out_projection, pointwise_in, pointwise_out)]
        in_plan = (whole_weight(0), [(0, width, 0, in_half, 0, 0)], width)
        plans = [
            (whole_weight(i), [(0, count, 0, part, 0, 0)], count)
            for i, count in enumerate((channels, width, conv_channels))
        ]

    keep, give = pl.pallas_call(
        lambda *r: assemble_kernel(slots, per_chunk, *r),
        out_shape=[like((owner_blocks, block_rows, part))] * 2,
        in_specs=[SMEM, SMEM] + [ANY] * (2 + 2 * CHUNKS),
        out_specs=[VMEM] * 2,
        scratch_shapes=[dma_sems(slots)],
        compiler_params=params(),
        name="assemble",
    )(place, table, slot_frames, theirs, *beside, *beyond)
    other = to_core(give)

    stream, q, kv = pl.pallas_call(
        lambda *r: qkv_kernel(*in_plan, *r),
        out_shape=[like((rows, width)), like((rows, channels)), like((2, rows, channels))],
        in_specs=[SMEM, VMEM, VMEM, VMEM] + [ANY] * len(in_arrays),
        out_specs=[VMEM] * 3,
        scratch_shapes=[
            pltpu.VMEM((2, width, in_half), bf16),
            pltpu.VMEM((rows, width), bf16),
            dma_sems(len(in_plan[0]) * len(in_plan[1])),
        ],
        compiler_params=params(),
        name="qkv",
    )(place, keep, other, gain_attention[None], *in_arrays)

    prior = lax.ppermute(kv, "tm", next_door)
    starts = utterance_start.reshape(rows, 1)

    mixed = pl.pallas_call(
        lambda *r: attention_kernel(frames, *r),
        out_shape=like((rows, channels)),
        in_specs=[SMEM] + [VMEM] * 4,
        out_specs=VMEM,
        scratch_shapes=[pltpu.VMEM((2 * rows, channels), bf16)] * 2,
        compiler_params=params(),
        name="attention",
    )(place, q, kv, prior, starts)

    if staged:
        mid_arrays = [rest_mine, rest_over[0], to_core(after(rest_over[0], mixed))]
    else:
        mid_arrays = last_arrays = rest_arrays

    middle, gated, edge = pl.pallas_call(
        lambda *r: gate_kernel(plans[0], plans[1], frames, *r),
        out_shape=[like((rows, width)), like((rows, conv_channels)), like((streams * EDGE, conv_channels))],
        in_specs=[SMEM, VMEM, VMEM, VMEM] + [ANY] * len(mid_arrays),
        out_specs=[VMEM] * 3,
        scratch_shapes=[
            pltpu.VMEM((2, channels, part), bf16),
            pltpu.VMEM((2, width, part), bf16),
            dma_sems(len(plans[0][0])),
            dma_sems(len(plans[1][0])),
        ],
        compiler_params=params(),
        name="gate",
    )(place, mixed, stream, gain_convolution[None], *mid_arrays)
    edge = lax.ppermute(edge, "tm", next_door)
    if staged:
        last_arrays = [rest_mine, rest_over[1], to_core(after(rest_over[1], gated))]

    lane_tiles = conv_channels // 128
    out = pl.pallas_call(
        lambda *r: conv_kernel(plans[2], frames, *r),
        out_shape=like((rows, width)),
        in_specs=[SMEM] + [VMEM] * 6 + [ANY] * len(last_arrays),
        out_specs=VMEM,
        scratch_shapes=[
            pltpu.VMEM((2, conv_channels, part), bf16),
            pltpu.VMEM((streams * lane_tiles, EDGE + frames, 128), f32),
            pltpu.VMEM((rows, conv_channels), f32),
            pltpu.VMEM((rows, 128), jnp.int32),
            dma_sems(len(plans[2][0])),
        ],
        compiler_params=params(),
        name="conv",
    )(place, gated, edge, middle, starts, depthwise, gain_depth[None], *last_arrays)
    return out.reshape(streams, frames, width)


def solution(mesh):
    in_specs = (
        P(("groups", "tm"), None, None),
        P(("groups", "tm")),
        P("groups", "tm"),
        P("tm", None),
        P("tm", None),
        P("tm", None),
        P(),
        P("tm", None),
        P(),
        P(),
        P(),
    )
    out_specs = P("groups", "tm", None)
    return jax.shard_map(shards, mesh=mesh, in_specs=in_specs, out_specs=out_specs, check_vma=False)
```
